32 devices in a mesh: ctx: 16 (over z, y, x), head: 2 (over core).
Axes of the slice: x: 2, y: 2, z: 4, core: 2. Of those that a mesh axis runs over, the one named last changes fastest.
Arguments:
- query_raw: bfloat16 [16384, 4096], P('ctx', 'head')
- key_raw: bfloat16 [16384, 1024], P('ctx', 'head')
- values: bfloat16 [16384, 1024], P('ctx', 'head'), may hold values from -6 to 6
- output_gradient: bfloat16 [16384, 4096], P('ctx', 'head'), may hold values from -6 to 6
- query_gain: float32 [4096], P('head'), may hold values from 0.5 to 3
- key_norm_gain: float32 [1024], P('head'), may hold values from 0.5 to 3
- block_docs: int32 [128], replicated, may hold values from 0 to 20, never falling along the last dimension, each value on 1 to 24 neighbouring positions
Outputs:
- attended: bfloat16 [16384, 4096], P('ctx', 'head')
- query_grad: bfloat16 [16384, 4096], P('ctx', 'head')
- key_raw_gradient: bfloat16 [16384, 1024], P('ctx', 'head')
- value_grad: bfloat16 [16384, 1024], P('ctx', 'head')
- query_gain_grad: float32 [4096], P('head')
- key_gain_grad: float32 [1024], P('head')
The draws below stay inside these ranges and needn't reach their ends.
Inputs may be any that keep to these rules, and one draw needn't show every extreme that they name: `block_docs`: document numbers never fall from one block to the next; each document covers 1 to 24 consecutive mask blocks, and one covers exactly 24.
All inputs are finite; a program needn't handle non-finite values.
Results may differ from the reference program's by a relative error of at most 0.024.
The reference program's roundings to bfloat16 on the way count: a program that leaves them out, or rounds other values in their place, can miss the bound.
Values may be sent and summed in bfloat16 or wider, within the bound.
No kernel may reach another device: no remote copies, remote signals or barrier semaphores. Data moves between devices by JAX's collectives and lax.ppermute only.
A program may use at most 128 MiB of HBM per device.

```python
import math
import jax
import jax.numpy as jnp
import numpy as np
from jax import lax

QUERY_HEADS = 32
KEY_VALUE_HEADS = 8
HEAD_SIZE = 128
WINDOW_REACH = 512
BLOCK = 128
MOST = 24
SEQUENCE_TOKENS = 16384
BLOCKS = 128
DOCS = 21


def qk_fields(key):
    pieces = jax.random.split(jax.random.fold_in(key, 41), 5)
    query_width = QUERY_HEADS * HEAD_SIZE
    key_span_width = KEY_VALUE_HEADS * HEAD_SIZE
    col_rise = 3.0
    row_top = 10.0
    query_base = jax.random.normal(pieces[0], (SEQUENCE_TOKENS, query_width), jnp.float32)
    key_base = jax.random.normal(pieces[1], (SEQUENCE_TOKENS, key_span_width), jnp.float32)
    row_scale = jnp.exp(jax.random.uniform(pieces[2], (SEQUENCE_TOKENS, 1), jnp.float32) * math.log(row_top))
    query_cols = jnp.exp(jnp.arange(query_width, dtype=jnp.float32) / (query_width - 1) * math.log(col_rise) + jax.random.uniform(pieces[3], (query_width,), jnp.float32) * math.log(10.0))
    key_cols = jnp.exp(jnp.arange(key_span_width, dtype=jnp.float32) / (key_span_width - 1) * math.log(col_rise) + jax.random.uniform(pieces[4], (key_span_width,), jnp.float32) * math.log(10.0))
    query = query_base * row_scale * query_cols
    keyfield = key_base * row_scale * key_cols
    return (query, keyfield)


def draw_query_raw(key, part):
    return qk_fields(key)[0].astype(jnp.bfloat16)


def draw_key_raw(key, part):
    return qk_fields(key)[1].astype(jnp.bfloat16)


def shard_levels(own_key, shape, cuts, smallest, top_value):
    level = 1.0
    for dim, shards_of in cuts:
        steps = jax.random.uniform(jax.random.fold_in(jax.random.fold_in(own_key, 6), dim), (shards_of,), jnp.float32, smallest / len(cuts), top_value / len(cuts))
        level = level * jnp.repeat(jnp.exp(steps), shape[dim] // shards_of).reshape((-1,) + (1,) * (len(shape) - 1 - dim))
    return level


def split_up(number_of, total, bound, skew):
    portions = [(1 << 20) // math.isqrt(standing ** skew) + 1 for standing in range(2, number_of + 1)]
    spare, holding = total - bound - (number_of - 1), [1] * (number_of - 1)
    while spare > 0:
        movable = [i for i in range(number_of - 1) if holding[i] < bound]
        mass, remaining = sum([portions[i] for i in movable]), spare
        for i in movable:
            addition = min(bound - holding[i], max(1, remaining * portions[i] // mass), spare)
            holding[i] = holding[i] + addition
            spare = spare - addition
    return np.array([bound] + holding)


def ragged_sizes(rng, count, total, most, slope):
    if count == 2:
        one = jax.random.randint(rng, (), max(1, total - most), min(most, total - 1) + 1)
        return jnp.stack([one, total - one])
    lengths = jnp.asarray(split_up(count, total, most, slope), jnp.int32)
    pairs = (count - 1) // 2
    source_of, receiver = lengths[1:1 + 2 * pairs:2], lengths[2:2 + 2 * pairs:2]
    slack = jnp.minimum(source_of - 1, most - receiver)
    passed = jax.random.randint(jax.random.fold_in(rng, 1), (pairs,), 0, 1 << 20) % (slack + 1)
    lengths = lengths.at[1:1 + 2 * pairs:2].set(source_of - passed).at[2:2 + 2 * pairs:2].set(receiver + passed)
    return lengths[jax.random.permutation(jax.random.fold_in(rng, 2), count)]


def normal_values(key, shape, width, most, cuts=(), kind=jnp.bfloat16):
    values = width * jax.random.normal(key, shape, jnp.float32)
    if cuts:
        values = values * shard_levels(key, shape, cuts, -0.22, 0.18)
    return jnp.clip(values, -most, most).astype(kind)


def setup_inputs(seed: int = 0) -> dict:
    seeds = jax.random.split(jax.random.key(seed), 8)
    query_raw = draw_query_raw(jax.random.fold_in(seeds[7], 71), 0)
    key_raw = draw_key_raw(jax.random.fold_in(seeds[7], 71), 0)
    values = normal_values(seeds[2], (SEQUENCE_TOKENS, KEY_VALUE_HEADS * HEAD_SIZE), 1.0, 6.0, ((0, 16), (1, 2)))
    output_gradient = normal_values(seeds[3], (SEQUENCE_TOKENS, QUERY_HEADS * HEAD_SIZE), 1.0, 6.0, ((0, 16), (1, 2)))
    query_gain = jnp.clip(0.5 + 2.5 * jax.random.uniform(seeds[4], (QUERY_HEADS * HEAD_SIZE,), jnp.float32) ** shard_levels(seeds[4], (QUERY_HEADS * HEAD_SIZE,), ((0, 2),), -0.2, 0.2), 0.5, 3.0)
    key_norm_gain = jnp.clip(0.5 + 2.5 * jax.random.uniform(seeds[5], (KEY_VALUE_HEADS * HEAD_SIZE,), jnp.float32) ** shard_levels(seeds[5], (KEY_VALUE_HEADS * HEAD_SIZE,), ((0, 2),), -0.2, 0.2), 0.5, 3.0)
    block_docs = jnp.searchsorted(jnp.cumsum(ragged_sizes(seeds[6], DOCS, BLOCKS, MOST, 2)), jnp.arange(BLOCKS), side="right").astype(jnp.int32)
    return {"query_raw": query_raw, "key_raw": key_raw, "values": values, "output_gradient": output_gradient, "query_gain": query_gain, "key_norm_gain": key_norm_gain, "block_docs": block_docs}


EPS = 1e-06
NEGATIVE = -1e+30

def rounded(tensor):
    return lax.optimization_barrier(tensor.astype(jnp.bfloat16)).astype(jnp.float32)

def rescale_each_row(raw, gain):
    floats = raw.astype(jnp.float32)
    scale_rows = lax.rsqrt(lax.optimization_barrier(jnp.mean(floats * floats, axis=1, keepdims=True)) + EPS)
    unit_rows = floats * scale_rows
    return (scale_rows, unit_rows, (unit_rows * gain).astype(jnp.bfloat16))

def norm_backward(grad, unit_rows, scale_rows, gain):
    scaled = grad * gain
    inner = lax.optimization_barrier(jnp.mean(scaled * unit_rows, axis=1, keepdims=True))
    return (scale_rows * (scaled - unit_rows * inner)).astype(jnp.bfloat16)

def reference(query_raw, key_raw, values, output_gradient, query_gain, key_norm_gain, block_docs):
    query_group_count = QUERY_HEADS // KEY_VALUE_HEADS
    stride_rows = min(512, WINDOW_REACH)
    softmax_scale = HEAD_SIZE ** (-0.5)
    query_scale, query_unit, query_normalized = rescale_each_row(query_raw, query_gain)
    key_inverse_scale, key_unit_rows, key_normalized = rescale_each_row(key_raw, key_norm_gain)
    key_padded = jnp.concatenate([jnp.zeros((WINDOW_REACH, KEY_VALUE_HEADS * HEAD_SIZE), jnp.bfloat16), key_normalized])
    value_padded = jnp.concatenate([jnp.zeros((WINDOW_REACH, KEY_VALUE_HEADS * HEAD_SIZE), jnp.bfloat16), values])
    doc_rows = jnp.repeat(block_docs, BLOCK)
    doc_pad = jnp.concatenate([jnp.full((WINDOW_REACH,), -1, jnp.int32), doc_rows])
    distance = jnp.arange(stride_rows, dtype=jnp.int32)[:, None] + WINDOW_REACH - jnp.arange(stride_rows + WINDOW_REACH, dtype=jnp.int32)[None, :]

    def attend(running, block_index):
        key_gradient_total, value_gradient_total = running
        leading_row = (block_index * stride_rows).astype(jnp.int32)
        key_total_count = stride_rows + WINDOW_REACH
        query_block = lax.dynamic_slice_in_dim(query_normalized, leading_row, stride_rows, 0).astype(jnp.float32).reshape(stride_rows, KEY_VALUE_HEADS, query_group_count, HEAD_SIZE)
        gradient_block = lax.dynamic_slice_in_dim(output_gradient, leading_row, stride_rows, 0).astype(jnp.float32).reshape(stride_rows, KEY_VALUE_HEADS, query_group_count, HEAD_SIZE)
        key_block = lax.dynamic_slice_in_dim(key_padded, leading_row, key_total_count, 0).astype(jnp.float32).reshape(key_total_count, KEY_VALUE_HEADS, HEAD_SIZE)
        value_block = lax.dynamic_slice_in_dim(value_padded, leading_row, key_total_count, 0).astype(jnp.float32).reshape(key_total_count, KEY_VALUE_HEADS, HEAD_SIZE)
        doc_query = lax.dynamic_slice_in_dim(doc_rows, leading_row, stride_rows, 0)
        doc_keys = lax.dynamic_slice_in_dim(doc_pad, leading_row, key_total_count, 0)
        visible = (distance >= 0) & (distance < WINDOW_REACH) & (doc_query[:, None] == doc_keys[None, :])
        scores = jnp.einsum('ighd,jgd->ghij', query_block, key_block) * softmax_scale
        row_max = lax.optimization_barrier(jnp.max(jnp.where(visible, scores, NEGATIVE), axis=-1, keepdims=True))
        expo = jnp.where(visible, jnp.exp(scores - row_max), 0.0)
        weights = expo / lax.optimization_barrier(jnp.sum(expo, axis=-1, keepdims=True))
        weights_low = rounded(weights)
        out_blk = jnp.einsum('ghij,jgd->ighd', weights_low, value_block).astype(jnp.bfloat16)
        delta = jnp.einsum('ighd,ighd->ghi', gradient_block, out_blk.astype(jnp.float32))
        dweights = jnp.einsum('ighd,jgd->ghij', gradient_block, value_block)
        dscores_low = rounded(weights * (dweights - delta[..., None]))
        dquery_blk = jnp.einsum('ghij,jgd->ighd', dscores_low, key_block) * softmax_scale
        key_gradient_block = jnp.einsum('ghij,ighd->jgd', dscores_low, query_block) * softmax_scale
        value_gradient_block = jnp.einsum('ghij,ighd->jgd', weights_low, gradient_block)
        present_key = lax.dynamic_slice_in_dim(key_gradient_total, leading_row, key_total_count, 0)
        key_gradient_total = lax.dynamic_update_slice_in_dim(key_gradient_total, present_key + key_gradient_block.reshape(key_total_count, KEY_VALUE_HEADS * HEAD_SIZE), leading_row, 0)
        present_value = lax.dynamic_slice_in_dim(value_gradient_total, leading_row, key_total_count, 0)
        value_gradient_total = lax.dynamic_update_slice_in_dim(value_gradient_total, present_value + value_gradient_block.reshape(key_total_count, KEY_VALUE_HEADS * HEAD_SIZE), leading_row, 0)
        return ((key_gradient_total, value_gradient_total), (out_blk.reshape(stride_rows, QUERY_HEADS * HEAD_SIZE), dquery_blk.reshape(stride_rows, QUERY_HEADS * HEAD_SIZE)))
    blank_start = jnp.zeros((SEQUENCE_TOKENS + WINDOW_REACH, KEY_VALUE_HEADS * HEAD_SIZE), jnp.float32)
    (key_gradient_total, value_gradient_total), (out_blocks, dquery_blocks) = lax.scan(attend, (blank_start, blank_start), jnp.arange(SEQUENCE_TOKENS // stride_rows, dtype=jnp.int32))
    attended = out_blocks.reshape(SEQUENCE_TOKENS, QUERY_HEADS * HEAD_SIZE)
    dquery = dquery_blocks.reshape(SEQUENCE_TOKENS, QUERY_HEADS * HEAD_SIZE)
    dkey = key_gradient_total[WINDOW_REACH:]
    value_grad = value_gradient_total[WINDOW_REACH:].astype(jnp.bfloat16)
    query_grad = norm_backward(dquery, query_unit, query_scale, query_gain)
    key_raw_gradient = norm_backward(dkey, key_unit_rows, key_inverse_scale, key_norm_gain)
    query_gain_grad = lax.optimization_barrier(jnp.sum(dquery * query_unit, axis=0))
    key_gain_grad = lax.optimization_barrier(jnp.sum(dkey * key_unit_rows, axis=0))
    return (attended, query_grad, key_raw_gradient, value_grad, query_gain_grad, key_gain_grad)
```

```python
import functools

import jax
import jax.numpy as jnp
from jax import lax
from jax.experimental import pallas as pl
from jax.experimental.pallas import tpu as pltpu
from jax.sharding import PartitionSpec as P

QUERY_HEADS = 32
KEY_VALUE_HEADS = 8
HEAD_SIZE = 128
WINDOW_REACH = 512
BLOCK = 128

EPS = 1e-06
NEGATIVE = -1e30
LOG2_E = 1.4426950408889634
SPAN = WINDOW_REACH + BLOCK
BACK = WINDOW_REACH // BLOCK


def stack_heads(tile, group):
    return jnp.concatenate(
        [tile[:, h * HEAD_SIZE : (h + 1) * HEAD_SIZE] for h in range(group)], axis=0
    )


def attention_tile(
    step,
    group,
    docs_ref,
    q_ref,
    scale_ref,
    gain,
    grad_ref,
    k_ref,
    v_ref,
    kt_ref,
    vt_ref,
    out_ref,
    dq_ref,
    dk_ref,
    dv_ref,
    dot_ref,
):
    softmax_scale = HEAD_SIZE ** (-0.5)
    cols = group * BLOCK
    row = step * BLOCK
    if not isinstance(step, int):
        row = pl.multiple_of(row, BLOCK)
    rows = pl.ds(row, BLOCK)
    window = pl.ds(row, SPAN)
    scale = jnp.transpose(jnp.broadcast_to(scale_ref[step], (BLOCK, BLOCK)))
    scale = jnp.concatenate([scale] * group, axis=1)
    unit = q_ref[rows, :].astype(jnp.float32) * scale
    queries = stack_heads((unit * gain).astype(jnp.bfloat16), group)
    grads = stack_heads(grad_ref[rows, :], group)
    grads_t = jnp.transpose(grads)
    keys = k_ref[window, :]
    vals = v_ref[window, :]

    seen = [docs_ref[step + j] == docs_ref[step + BACK] for j in range(BACK)]
    key_pos = lax.broadcasted_iota(jnp.int32, (BLOCK, BLOCK), 0)
    query_pos = lax.broadcasted_iota(jnp.int32, (BLOCK, BLOCK), 1)
    causal = jnp.concatenate([key_pos <= query_pos] * group, axis=1)

    scores = lax.dot_general(
        keys, queries, (((1,), (1,)), ((), ())), preferred_element_type=jnp.float32
    )
    part = [scores[j * BLOCK : (j + 1) * BLOCK] for j in range(BACK + 1)]
    edge = jnp.where(causal, part[BACK], part[0] + jnp.where(seen[0], 0.0, NEGATIVE))
    top = jnp.max(edge, axis=0, keepdims=True)
    for j in range(1, BACK):
        top = jnp.maximum(
            top,
            jnp.max(part[j], axis=0, keepdims=True) + jnp.where(seen[j], 0.0, NEGATIVE),
        )
    factor = softmax_scale * LOG2_E
    expo = [jnp.exp2((edge - top) * factor)]
    for j in range(1, BACK):
        expo.append(jnp.exp2((part[j] - (top + jnp.where(seen[j], 0.0, -NEGATIVE))) * factor))
    total = jnp.sum(expo[0], axis=0, keepdims=True)
    for j in range(1, BACK):
        total = total + jnp.sum(expo[j], axis=0, keepdims=True)
    inverse = 1.0 / total
    weights = [e * inverse for e in expo]

    def split_edge(parts):
        zero = jnp.zeros_like(parts[0])
        return jnp.concatenate(
            [jnp.where(causal, zero, parts[0])]
            + parts[1:]
            + [jnp.where(causal, parts[0], zero)],
            axis=0,
        ).astype(jnp.bfloat16)

    weights_low = split_edge(weights)
    out_t = jnp.dot(
        vt_ref[:, window], weights_low, preferred_element_type=jnp.float32
    ).astype(jnp.bfloat16)
    delta = jnp.sum(
        grads_t.astype(jnp.float32) * out_t.astype(jnp.float32), axis=0, keepdims=True
    )
    out = jnp.transpose(out_t)
    for h in range(group):
        out_ref[rows, h * HEAD_SIZE : (h + 1) * HEAD_SIZE] = out[h * BLOCK : (h + 1) * BLOCK]

    dweights = jnp.dot(vals, grads_t, preferred_element_type=jnp.float32)
    dpart = [dweights[j * BLOCK : (j + 1) * BLOCK] for j in range(BACK + 1)]
    dpart[0] = jnp.where(causal, dpart[BACK], dpart[0])
    dscores_low = split_edge([weights[j] * (dpart[j] - delta) for j in range(BACK)])

    dv_ref[window, :] += jnp.dot(weights_low, grads, preferred_element_type=jnp.float32)
    dk_ref[window, :] += (
        jnp.dot(dscores_low, queries, preferred_element_type=jnp.float32) * softmax_scale
    )
    dquery = (
        jnp.transpose(
            jnp.dot(kt_ref[:, window], dscores_low, preferred_element_type=jnp.float32)
        )
        * softmax_scale
    )
    dquery = jnp.concatenate([dquery[h * BLOCK : (h + 1) * BLOCK] for h in range(group)], axis=1)
    dq_ref[rows, :] = dquery
    gained = dquery * unit
    inner = gained * gain
    folded = inner[:, :HEAD_SIZE]
    for h in range(1, group):
        folded = folded + inner[:, h * HEAD_SIZE : (h + 1) * HEAD_SIZE]
    dot_ref[step] = jnp.sum(jnp.transpose(folded), axis=0, keepdims=True)
    return jnp.sum(gained, axis=0, keepdims=True)


def attention_kernel(
    group,
    docs_ref,
    q_ref,
    scale_ref,
    gain_ref,
    grad_ref,
    k_ref,
    v_ref,
    out_ref,
    dq_ref,
    dk_ref,
    dv_ref,
    dot_ref,
    gain_grad_ref,
    kt_ref,
    vt_ref,
):
    kt_ref[...] = jnp.transpose(k_ref[...])
    vt_ref[...] = jnp.transpose(v_ref[...])
    dk_ref[...] = jnp.zeros_like(dk_ref)
    dv_ref[...] = jnp.zeros_like(dv_ref)
    gain = gain_ref[...]
    steps = q_ref.shape[0] // BLOCK

    def body(step, total):
        return total + attention_tile(
            step, group, docs_ref, q_ref, scale_ref, gain, grad_ref, k_ref, v_ref,
            kt_ref, vt_ref, out_ref, dq_ref, dk_ref, dv_ref, dot_ref,
        )

    total = jnp.zeros((1, group * HEAD_SIZE), jnp.float32)
    if UNROLL:
        for step in range(steps):
            total = body(step, total)
    else:
        total = lax.fori_loop(0, steps, body, total)
    gain_grad_ref[...] = total


UNROLL = False


def attention(docs, query_raw, query_scale, query_gain, output_gradient, keys, values, first, count):
    query_cols = query_raw.shape[1]
    key_rows, key_cols = keys.shape
    kv_heads = key_cols // HEAD_SIZE
    group = query_cols // key_cols
    width = group * HEAD_SIZE
    steps = count // BLOCK
    lead = first // count
    queries_spec = pl.BlockSpec((count, width), lambda g: (lead, g))
    rows_spec = pl.BlockSpec((count, width), lambda g: (0, g))
    keys_spec = pl.BlockSpec((key_rows, HEAD_SIZE), lambda g: (0, g))
    f32 = jnp.float32
    return pl.pallas_call(
        functools.partial(attention_kernel, group),
        grid=(kv_heads,),
        in_specs=[
            pl.BlockSpec(memory_space=pltpu.SMEM),
            queries_spec,
            pl.BlockSpec((steps, 1, BLOCK), lambda g: (lead, 0, 0)),
            pl.BlockSpec((1, width), lambda g: (0, g)),
            queries_spec,
            keys_spec,
            keys_spec,
        ],
        out_specs=[
            rows_spec,
            rows_spec,
            keys_spec,
            keys_spec,
            pl.BlockSpec((None, steps, 1, BLOCK), lambda g: (g, 0, 0, 0)),
            pl.BlockSpec((1, width), lambda g: (0, g)),
        ],
        out_shape=[
            jax.ShapeDtypeStruct((count, query_cols), jnp.bfloat16),
            jax.ShapeDtypeStruct((count, query_cols), f32),
            jax.ShapeDtypeStruct((key_rows, key_cols), f32),
            jax.ShapeDtypeStruct((key_rows, key_cols), f32),
            jax.ShapeDtypeStruct((kv_heads, steps, 1, BLOCK), f32),
            jax.ShapeDtypeStruct((1, query_cols), f32),
        ],
        scratch_shapes=[
            pltpu.VMEM((HEAD_SIZE, key_rows), jnp.bfloat16),
            pltpu.VMEM((HEAD_SIZE, key_rows), jnp.bfloat16),
        ],
        cost_estimate=pl.CostEstimate(
            flops=12 * count * query_cols * SPAN,
            bytes_accessed=count * query_cols * 10 + key_rows * key_cols * 12,
            transcendentals=count * query_cols // HEAD_SIZE * WINDOW_REACH,
        ),
        name="attention",
    )(docs, query_raw, query_scale, query_gain, output_gradient, keys, values)


def from_behind(array, axis, by):
    peers = lax.axis_size(axis)
    pairs = [(i, i + by) for i in range(peers) if 0 <= i + by < peers]
    return lax.ppermute(array, axis, pairs)


def sum_over(array, axis):
    peers = lax.axis_size(axis)
    if peers & (peers - 1):
        return lax.psum(array, axis)
    step = 1
    while step < peers:
        array = array + lax.ppermute(array, axis, [(i, i ^ step) for i in range(peers)])
        step *= 2
    return array


def local(query_raw, key_raw, values, output_gradient, query_gain, key_norm_gain, block_docs):
    f32 = jnp.float32
    tok_rows, query_cols = query_raw.shape
    key_cols = key_raw.shape[1]
    tail = tok_rows - WINDOW_REACH
    halo = from_behind(
        jnp.concatenate([key_raw[tail:], values[tail:]], axis=1), "ctx", 1
    )
    query_float = query_raw.astype(f32)
    key_float = key_raw.astype(f32)
    query_sq, key_sq = lax.psum(
        (jnp.sum(query_float * query_float, axis=1), jnp.sum(key_float * key_float, axis=1)),
        "head",
    )
    query_scale = lax.rsqrt(query_sq / (QUERY_HEADS * HEAD_SIZE) + EPS)
    key_scale = lax.rsqrt(key_sq / (KEY_VALUE_HEADS * HEAD_SIZE) + EPS)
    halo_scale = from_behind(key_scale[tail:], "ctx", 1)

    key_unit = key_float * key_scale[:, None]
    keys = (key_unit * key_norm_gain).astype(jnp.bfloat16)
    first_block = lax.axis_index("ctx") * (tok_rows // BLOCK)
    docs = lax.dynamic_slice_in_dim(
        jnp.concatenate([jnp.full((BACK,), -1, jnp.int32), block_docs]),
        first_block,
        BACK + tok_rows // BLOCK,
        0,
    )
    scale_rows = query_scale.reshape(tok_rows // BLOCK, 1, BLOCK)
    gain_row = query_gain.reshape(1, query_cols)
    later = [
        attention(
            docs[BACK + first // BLOCK - BACK + 0 :],
            query_raw,
            scale_rows,
            gain_row,
            output_gradient,
            keys[first - WINDOW_REACH : first + WINDOW_REACH],
            values[first - WINDOW_REACH : first + WINDOW_REACH],
            first,
            WINDOW_REACH,
        )
        for first in range(WINDOW_REACH, tok_rows, WINDOW_REACH)
    ]

    halo_unit = halo[:, :key_cols].astype(f32) * halo_scale[:, None]
    halo_keys = (halo_unit * key_norm_gain).astype(jnp.bfloat16)
    head = attention(
        docs,
        query_raw,
        scale_rows,
        gain_row,
        output_gradient,
        jnp.concatenate([halo_keys, keys[:WINDOW_REACH]]),
        jnp.concatenate([halo[:, key_cols:], values[:WINDOW_REACH]]),
        0,
        WINDOW_REACH,
    )
    parts = [head] + later
    back_key, back_value = head[2][:WINDOW_REACH], head[3][:WINDOW_REACH]
    back = from_behind(
        jnp.concatenate([back_key, back_value], axis=1).astype(jnp.bfloat16), "ctx", -1
    )

    def own(which):
        chunks = []
        for index, part in enumerate(parts):
            chunk = part[which][WINDOW_REACH:]
            if index + 1 < len(parts):
                chunk = chunk + parts[index + 1][which][:WINDOW_REACH]
            chunks.append(chunk)
        return jnp.concatenate(chunks)

    attended = jnp.concatenate([part[0] for part in parts])
    dquery = jnp.concatenate([part[1] for part in parts])
    dkey = own(2)
    dvalue = own(3)
    query_dot = jnp.concatenate(
        [jnp.sum(part[4], axis=0).reshape(WINDOW_REACH) for part in parts]
    )
    key_dot = jnp.sum(dkey * key_norm_gain * key_unit, axis=1)
    halo_dot = jnp.sum(back_key * key_norm_gain * halo_unit, axis=1)
    query_dot, key_dot, halo_dot = lax.psum((query_dot, key_dot, halo_dot), "head")
    back_dot = from_behind(halo_dot, "ctx", -1)
    query_gain_part = sum(part[5] for part in parts)[0]
    key_gain_part = jnp.sum(dkey * key_unit, axis=0) + jnp.sum(back_key * halo_unit, axis=0)
    gains = sum_over(jnp.concatenate([query_gain_part, key_gain_part]), "ctx")
    query_gain_grad = gains[:query_cols]
    key_gain_grad = gains[query_cols:]

    query_unit = query_float * query_scale[:, None]
    query_grad = (
        query_scale[:, None]
        * (dquery * query_gain - query_unit * (query_dot / (QUERY_HEADS * HEAD_SIZE))[:, None])
    ).astype(jnp.bfloat16)

    dkey = jnp.concatenate([dkey[:tail], dkey[tail:] + back[:, :key_cols].astype(f32)])
    value_grad = jnp.concatenate(
        [dvalue[:tail], dvalue[tail:] + back[:, key_cols:].astype(f32)]
    ).astype(jnp.bfloat16)
    key_dot = jnp.concatenate([key_dot[:tail], key_dot[tail:] + back_dot])
    key_raw_gradient = (
        key_scale[:, None]
        * (
            dkey * key_norm_gain
            - key_unit * (key_dot / (KEY_VALUE_HEADS * HEAD_SIZE))[:, None]
        )
    ).astype(jnp.bfloat16)
    return (attended, query_grad, key_raw_gradient, value_grad, query_gain_grad, key_gain_grad)


def solution(mesh):
    placed = (
        P("ctx", "head"),
        P("ctx", "head"),
        P("ctx", "head"),
        P("ctx", "head"),
        P("head"),
        P("head"),
        P(),
    )
    return jax.shard_map(
        local,
        mesh=mesh,
        in_specs=placed,
        out_specs=(
            P("ctx", "head"),
            P("ctx", "head"),
            P("ctx", "head"),
            P("ctx", "head"),
            P("head"),
            P("head"),
        ),
        check_vma=False,
    )
```

```python
import functools

import jax
import jax.numpy as jnp
from jax import lax
from jax.experimental import pallas as pl
from jax.experimental.pallas import tpu as pltpu
from jax.sharding import PartitionSpec as P


QUERY_HEADS = 32
KEY_VALUE_HEADS = 8
HEAD_SIZE = 128
WINDOW_REACH = 512
BLOCK = 128

EPS = 1e-06
NEGATIVE = -1e30
LOG2_E = 1.4426950408889634
SOFTMAX_SCALE = HEAD_SIZE ** (-0.5)
SPAN = WINDOW_REACH + BLOCK
BACK = WINDOW_REACH // BLOCK
PAIR = 2 * HEAD_SIZE


def side_by_side(stacked, group):
    return jnp.concatenate([stacked[h * BLOCK : (h + 1) * BLOCK] for h in range(group)], axis=1)


def on_top(tile, group):
    return jnp.concatenate(
        [tile[:, h * HEAD_SIZE : (h + 1) * HEAD_SIZE] for h in range(group)], axis=0
    )


def as_columns(row):
    return jnp.transpose(jnp.broadcast_to(row, (BLOCK, BLOCK)))


def query_scale(summed):
    return lax.rsqrt(summed * (1.0 / (QUERY_HEADS * HEAD_SIZE)) + EPS)


def key_scale(summed):
    return lax.rsqrt(summed * (1.0 / (KEY_VALUE_HEADS * HEAD_SIZE)) + EPS)


def fold_rows(tile):
    folded = tile[:, :HEAD_SIZE]
    for h in range(1, tile.shape[1] // HEAD_SIZE):
        folded = folded + tile[:, h * HEAD_SIZE : (h + 1) * HEAD_SIZE]
    return jnp.sum(jnp.transpose(folded), axis=0, keepdims=True)


def attention_kernel(group, chunk, chunks, passed, begun, *refs):
    (
        docs_ref,
        q_ref,
        q_scale_ref,
        q_gain_ref,
        grad_ref,
        k_lo_ref,
        k_hi_ref,
        lo_scale_ref,
        hi_scale_ref,
        k_gain_ref,
        v_lo_ref,
        v_hi_ref,
    ) = refs[:12]
    refs = refs[12:]
    prior_gain_ref, prior_dots_ref = None, None
    if begun[0]:
        prior_gain_ref, refs = refs[0], refs[1:]
    if begun[1]:
        prior_dots_ref, refs = refs[0], refs[1:]
    refs = refs[passed:]
    (
        out_ref,
        dq_ref,
        hi_ref,
        gain_grad_ref,
        dots_ref,
        lo_ref,
        k_scr,
        v_scr,
        kt_scr,
        vt_scr,
        unit_scr,
        dk_scr,
        dv_scr,
    ) = refs
    f32, bf16 = jnp.float32, jnp.bfloat16
    q_gain = q_gain_ref[...]
    k_gain = k_gain_ref[...]

    for half, (raw_ref, scale_ref, val_ref) in enumerate(
        ((k_lo_ref, lo_scale_ref, v_lo_ref), (k_hi_ref, hi_scale_ref, v_hi_ref))
    ):
        for j in range(BACK):
            src = slice(j * BLOCK, (j + 1) * BLOCK)
            dst = slice((half * BACK + j) * BLOCK, (half * BACK + j + 1) * BLOCK)
            unit = raw_ref[src, :].astype(f32) * as_columns(key_scale(scale_ref[j]))
            unit_scr[dst, :] = unit
            norm = (unit * k_gain).astype(bf16)
            k_scr[dst, :] = norm
            kt_scr[:, dst] = jnp.transpose(norm)
            vals = val_ref[src, :]
            v_scr[dst, :] = vals
            vt_scr[:, dst] = jnp.transpose(vals)
    dk_scr[...] = jnp.zeros_like(dk_scr)
    dv_scr[...] = jnp.zeros_like(dv_scr)

    def mask():
        key_pos = lax.broadcasted_iota(jnp.int32, (BLOCK, BLOCK), 0)
        query_pos = lax.broadcasted_iota(jnp.int32, (BLOCK, BLOCK), 1)
        return jnp.concatenate([key_pos <= query_pos] * group, axis=1)

    def split_edge(parts):
        causal = mask()
        zero = jnp.zeros_like(parts[0])
        return jnp.concatenate(
            [jnp.where(causal, zero, parts[0])]
            + parts[1:]
            + [jnp.where(causal, parts[0], zero)],
            axis=0,
        ).astype(bf16)

    def forward(step):
        rows = slice(step * BLOCK, (step + 1) * BLOCK)
        window = slice(step * BLOCK, step * BLOCK + SPAN)
        scale = jnp.concatenate([as_columns(query_scale(q_scale_ref[step]))] * group, axis=1)
        unit = q_ref[rows, :].astype(f32) * scale
        queries = on_top((unit * q_gain).astype(bf16), group)
        place = chunk * BACK + step
        seen = [docs_ref[place + j] == docs_ref[place + BACK] for j in range(BACK)]
        scores = lax.dot_general(
            k_scr[window, :], queries, (((1,), (1,)), ((), ())), preferred_element_type=f32
        )
        part = [scores[j * BLOCK : (j + 1) * BLOCK] for j in range(BACK + 1)]
        edge = jnp.where(mask(), part[BACK], part[0] + jnp.where(seen[0], 0.0, NEGATIVE))
        top = jnp.max(edge, axis=0, keepdims=True)
        for j in range(1, BACK):
            top = jnp.maximum(
                top,
                jnp.max(part[j], axis=0, keepdims=True) + jnp.where(seen[j], 0.0, NEGATIVE),
            )
        factor = SOFTMAX_SCALE * LOG2_E
        expo = [jnp.exp2((edge - top) * factor)]
        for j in range(1, BACK):
            lift = top + jnp.where(seen[j], 0.0, -NEGATIVE)
            expo.append(jnp.exp2((part[j] - lift) * factor))
        total = jnp.sum(expo[0], axis=0, keepdims=True)
        for j in range(1, BACK):
            total = total + jnp.sum(expo[j], axis=0, keepdims=True)
        inverse = 1.0 / total
        weights = [e * inverse for e in expo]
        return queries, weights

    def backward(step, state):
        queries, weights = state
        rows = slice(step * BLOCK, (step + 1) * BLOCK)
        window = slice(step * BLOCK, step * BLOCK + SPAN)
        grads = on_top(grad_ref[rows, :], group)
        grads_t = jnp.transpose(grads)
        weights_low = split_edge(weights)
        out_t = jnp.dot(vt_scr[:, window], weights_low, preferred_element_type=f32).astype(bf16)
        delta = jnp.sum(grads_t.astype(f32) * out_t.astype(f32), axis=0, keepdims=True)
        out_ref[rows, :] = side_by_side(jnp.transpose(out_t), group)
        dweights = jnp.dot(v_scr[window, :], grads_t, preferred_element_type=f32)
        dpart = [dweights[j * BLOCK : (j + 1) * BLOCK] for j in range(BACK + 1)]
        dpart[0] = jnp.where(mask(), dpart[BACK], dpart[0])
        dscores_low = split_edge([weights[j] * (dpart[j] - delta) for j in range(BACK)])
        dv_scr[window, :] += jnp.dot(weights_low, grads, preferred_element_type=f32)
        dk_scr[window, :] += jnp.dot(dscores_low, queries, preferred_element_type=f32)
        dq_t = jnp.dot(kt_scr[:, window], dscores_low, preferred_element_type=f32)
        dquery = side_by_side(jnp.transpose(dq_t), group) * SOFTMAX_SCALE
        scale = jnp.concatenate([as_columns(query_scale(q_scale_ref[step]))] * group, axis=1)
        unit = q_ref[rows, :].astype(f32) * scale
        gained = dquery * q_gain
        dq_ref[rows, :] = gained.astype(bf16)
        query_dots.append(fold_rows(gained * unit))
        return jnp.sum(dquery * unit, axis=0, keepdims=True)

    steps = q_ref.shape[0] // BLOCK
    query_dots = []
    total = jnp.zeros((1, group * HEAD_SIZE), f32)
    if PIPELINE:
        state = forward(0)
        for step in range(steps):
            following = forward(step + 1) if step + 1 < steps else None
            total = total + backward(step, state)
            state = following
    else:
        for step in range(steps):
            total = total + backward(step, forward(step))
    width = group * HEAD_SIZE

    key_total = jnp.zeros((1, HEAD_SIZE), f32)
    key_dots = []
    for half, ref in enumerate((lo_ref, hi_ref)):
        for j in range(BACK):
            dst = slice(j * BLOCK, (j + 1) * BLOCK)
            src = slice((half * BACK + j) * BLOCK, (half * BACK + j + 1) * BLOCK)
            dkey = dk_scr[src, :] * SOFTMAX_SCALE
            gained = dkey * unit_scr[src, :]
            key_total = key_total + jnp.sum(gained, axis=0, keepdims=True)
            key_dots.append(fold_rows(gained * k_gain))
            ref[dst, :HEAD_SIZE] = dkey.astype(ref.dtype)
            ref[dst, HEAD_SIZE:] = dv_scr[src, :].astype(ref.dtype)
    if prior_gain_ref is not None:
        total = total + prior_gain_ref[:, :width]
        key_total = key_total + prior_gain_ref[:, width:]
    gain_grad_ref[:, :width] = total
    gain_grad_ref[:, width:] = key_total

    @pl.when(pl.program_id(0) == 0)
    def _():
        if prior_dots_ref is None:
            dots_ref[...] = jnp.zeros_like(dots_ref)
        else:
            dots_ref[...] = prior_dots_ref[...]

    for step in range(steps):
        dots_ref[chunk * BACK + step] += query_dots[step]
    for j in range(0 if chunk else BACK, 2 * BACK):
        dots_ref[(chunks + chunk - 1) * BACK + j] += key_dots[j]


PIPELINE = True


def attention(
    docs, q_raw, q_scale, q_gain, grad, lo, hi, k_gain, passed, chunk, heads, own_lo, begun
):
    tok_rows, query_cols = q_raw.shape
    key_cols = k_gain.shape[1]
    group = query_cols // key_cols
    width = group * HEAD_SIZE
    lowest, count = heads
    f32, bf16 = jnp.float32, jnp.bfloat16
    rows_spec = pl.BlockSpec((WINDOW_REACH, width), lambda g: (chunk, lowest + g))
    scale_spec = lambda block: pl.BlockSpec((BACK, 1, BLOCK), lambda g: (block, 0, 0))
    key_spec = lambda block, col: pl.BlockSpec((WINDOW_REACH, HEAD_SIZE), lambda g: (block, col + g))
    pair_spec = pl.BlockSpec((WINDOW_REACH, PAIR), lambda g: (0, lowest + g))
    own_pair_spec = pl.BlockSpec((WINDOW_REACH, PAIR), lambda g: (0, g))
    gain_spec = pl.BlockSpec((1, width + HEAD_SIZE), lambda g: (0, lowest + g))
    blocks = tok_rows // BLOCK
    whole_spec = pl.BlockSpec((2 * blocks, 1, BLOCK), lambda g: (0, 0, 0))
    operands = [docs, q_raw, q_scale, q_gain, grad, lo[0], hi[0], lo[1], hi[1], k_gain, lo[5], hi[5]]
    in_specs = [
        pl.BlockSpec(memory_space=pltpu.SMEM),
        rows_spec,
        scale_spec(chunk),
        pl.BlockSpec((1, width), lambda g: (0, lowest + g)),
        rows_spec,
        key_spec(lo[2], lo[3]),
        key_spec(hi[2], hi[3]),
        scale_spec(lo[2]),
        scale_spec(hi[2]),
        pl.BlockSpec((1, HEAD_SIZE), lambda g: (0, lowest + g)),
        key_spec(lo[2], lo[4]),
        key_spec(hi[2], hi[4]),
    ]
    outs = [
        (rows_spec, (tok_rows, query_cols), bf16),
        (rows_spec, (tok_rows, query_cols), bf16),
        (pair_spec, (WINDOW_REACH, 2 * key_cols), bf16),
        (gain_spec, (1, query_cols + key_cols), f32),
        (whole_spec, (2 * blocks, 1, BLOCK), f32),
        (own_pair_spec, (WINDOW_REACH, count * PAIR), bf16)
        if own_lo
        else (pair_spec, (WINDOW_REACH, 2 * key_cols), bf16),
    ]
    aliases, extra = {}, []
    for index, spec in ((3, gain_spec), (4, whole_spec)):
        if begun[index - 3]:
            aliases[len(operands)] = index
            operands.append(passed[index])
            in_specs.append(spec)
    for index, array in enumerate(passed):
        if array is not None and index not in aliases.values():
            aliases[len(operands) + len(extra)] = index
            extra.append(array)
    return pl.pallas_call(
        functools.partial(
            attention_kernel, group, chunk, blocks // BACK, len(extra), begun
        ),
        grid=(count,),
        in_specs=in_specs + [pl.BlockSpec(memory_space=pl.ANY)] * len(extra),
        out_specs=[o[0] for o in outs],
        out_shape=[jax.ShapeDtypeStruct(o[1], o[2]) for o in outs],
        input_output_aliases=aliases,
        scratch_shapes=[
            pltpu.VMEM((2 * WINDOW_REACH, HEAD_SIZE), bf16),
            pltpu.VMEM((2 * WINDOW_REACH, HEAD_SIZE), bf16),
            pltpu.VMEM((HEAD_SIZE, 2 * WINDOW_REACH), bf16),
            pltpu.VMEM((HEAD_SIZE, 2 * WINDOW_REACH), bf16),
            pltpu.VMEM((2 * WINDOW_REACH, HEAD_SIZE), f32),
            pltpu.VMEM((2 * WINDOW_REACH, HEAD_SIZE), f32),
            pltpu.VMEM((2 * WINDOW_REACH, HEAD_SIZE), f32),
        ],
        cost_estimate=pl.CostEstimate(
            flops=12 * WINDOW_REACH * count * width * SPAN,
            bytes_accessed=WINDOW_REACH * count * (8 * width + 16 * HEAD_SIZE),
            transcendentals=WINDOW_REACH * count * group * WINDOW_REACH,
        ),
        name="halo_attention" if own_lo else "attention",
    )(*operands, *extra)


def back_dot_kernel(raw_ref, scale_ref, gain_ref, dots_ref, *refs):
    backs, out_ref = refs[:-1], refs[-1]
    out_ref[...] = dots_ref[...]
    first = dots_ref.shape[0] - BACK
    for j in range(BACK):
        rows = slice(j * BLOCK, (j + 1) * BLOCK)
        index = first + j
        total = jnp.zeros((BLOCK, BLOCK), jnp.float32)
        head = 0
        for back in backs:
            for h in range(back.shape[1] // PAIR):
                cols = slice(head * HEAD_SIZE, (head + 1) * HEAD_SIZE)
                grad = back[rows, h * PAIR : h * PAIR + HEAD_SIZE].astype(jnp.float32)
                total = total + grad * gain_ref[:, cols] * raw_ref[rows, cols].astype(jnp.float32)
                head += 1
        out_ref[index] = dots_ref[index] + fold_rows(total * as_columns(key_scale(scale_ref[j])))


def add_back_dots(key_raw, k_scale, k_gain, dots, backs):
    tok_rows, key_cols = key_raw.shape
    last = tok_rows // WINDOW_REACH - 1
    return pl.pallas_call(
        back_dot_kernel,
        grid=(1,),
        in_specs=[
            pl.BlockSpec((WINDOW_REACH, key_cols), lambda g: (last, 0)),
            pl.BlockSpec((BACK, 1, BLOCK), lambda g: (last, 0, 0)),
            pl.BlockSpec((1, key_cols), lambda g: (0, 0)),
            pl.BlockSpec(dots.shape, lambda g: (0, 0, 0)),
        ]
        + [pl.BlockSpec(back.shape, lambda g: (0, 0)) for back in backs],
        out_specs=pl.BlockSpec(dots.shape, lambda g: (0, 0, 0)),
        out_shape=jax.ShapeDtypeStruct(dots.shape, jnp.float32),
        name="back_dots",
    )(key_raw, k_scale, k_gain, dots, *backs)


def finish_kernel(group, chunks, passed, *refs):
    f32 = jnp.float32
    (u_ref, q_ref, q_scale_ref, k_ref, k_scale_ref, k_gain_ref, dots_ref), refs = refs[:7], refs[7:]
    highs, refs = refs[:chunks], refs[chunks:]
    lows, refs = refs[: chunks - 1], refs[chunks - 1 :]
    back, refs = refs[0], refs[1 + passed :]
    q_out, k_out, v_out, qa_scr, qd_scr, ka_scr, kd_scr = refs
    g = pl.program_id(0)
    blocks = chunks * BACK

    @pl.when(g == 0)
    def _():
        for b in range(blocks):
            rows = slice(b * BLOCK, (b + 1) * BLOCK)
            dot = dots_ref[b]
            qa_scr[rows, :] = as_columns(query_scale(q_scale_ref[b]))
            qd_scr[rows, :] = as_columns(dot * (1.0 / (QUERY_HEADS * HEAD_SIZE)))
            dot = dots_ref[blocks + b]
            ka_scr[rows, :] = as_columns(key_scale(k_scale_ref[b]))
            kd_scr[rows, :] = as_columns(dot * (1.0 / (KEY_VALUE_HEADS * HEAD_SIZE)))

    for b in range(blocks):
        rows = slice(b * BLOCK, (b + 1) * BLOCK)
        scale, dot = qa_scr[rows, :], qd_scr[rows, :]
        for h in range(group):
            cols = slice(h * HEAD_SIZE, (h + 1) * HEAD_SIZE)
            unit = q_ref[rows, cols].astype(f32) * scale
            q_out[rows, cols] = (scale * (u_ref[rows, cols].astype(f32) - unit * dot)).astype(
                q_out.dtype
            )
    for b in range(blocks):
        rows = slice(b * BLOCK, (b + 1) * BLOCK)
        chunk, j = divmod(b, BACK)
        src = slice(j * BLOCK, (j + 1) * BLOCK)
        grad = highs[chunk][src, :].astype(f32)
        if chunk < chunks - 1:
            grad = grad + lows[chunk][src, :].astype(f32)
        else:
            grad = grad + back[src, :].astype(f32)
        scale, dot = ka_scr[rows, :], kd_scr[rows, :]
        unit = k_ref[rows, :].astype(f32) * scale
        k_out[rows, :] = (
            scale * (grad[:, :HEAD_SIZE] * k_gain_ref[...] - unit * dot)
        ).astype(k_out.dtype)
        v_out[rows, :] = grad[:, HEAD_SIZE:].astype(v_out.dtype)


def finish(scaled, q_raw, q_scale, key_raw, k_scale, k_gain, dots, highs, lows, back, heads, passed):
    tok_rows, query_cols = q_raw.shape
    key_cols = key_raw.shape[1]
    group = query_cols // key_cols
    chunks = tok_rows // WINDOW_REACH
    lowest, count = heads
    queries = pl.BlockSpec((tok_rows, group * HEAD_SIZE), lambda g: (0, lowest + g))
    keys = pl.BlockSpec((tok_rows, HEAD_SIZE), lambda g: (0, lowest + g))
    pairs = pl.BlockSpec((WINDOW_REACH, PAIR), lambda g: (0, lowest + g))
    fixed = lambda array: pl.BlockSpec(array.shape, lambda g: (0, 0, 0))
    bf16 = jnp.bfloat16
    operands = [scaled, q_raw, q_scale, key_raw, k_scale, k_gain, dots, *highs, *lows, back]
    return pl.pallas_call(
        functools.partial(finish_kernel, group, chunks, len(passed)),
        grid=(count,),
        in_specs=[
            queries,
            queries,
            fixed(q_scale),
            keys,
            fixed(k_scale),
            pl.BlockSpec((1, HEAD_SIZE), lambda g: (0, lowest + g)),
            fixed(dots),
        ]
        + [pairs] * (len(highs) + len(lows))
        + [pl.BlockSpec((WINDOW_REACH, PAIR), lambda g: (0, g))]
        + [pl.BlockSpec(memory_space=pl.ANY)] * len(passed),
        out_specs=[queries, keys, keys],
        out_shape=[
            jax.ShapeDtypeStruct((tok_rows, query_cols), bf16),
            jax.ShapeDtypeStruct((tok_rows, key_cols), bf16),
            jax.ShapeDtypeStruct((tok_rows, key_cols), bf16),
        ],
        input_output_aliases={len(operands) + i: i for i in range(len(passed))},
        scratch_shapes=[pltpu.VMEM((tok_rows, HEAD_SIZE), jnp.float32)] * 4,
        cost_estimate=pl.CostEstimate(
            flops=8 * tok_rows * count * group * HEAD_SIZE,
            bytes_accessed=tok_rows * count * HEAD_SIZE * (6 * group + 12),
            transcendentals=0,
        ),
        name="finish",
    )(*operands, *passed)


def square_kernel(q_ref, k_ref, q_out, k_out):
    for ref, out in ((q_ref, q_out), (k_ref, k_out)):
        for j in range(ref.shape[0] // BLOCK):
            tile = ref[j * BLOCK : (j + 1) * BLOCK, :].astype(jnp.float32)
            out[j] = fold_rows(tile * tile)


def row_squares(q_raw, key_raw):
    tok_rows = q_raw.shape[0]
    step = 2 * BLOCK
    blocks = tok_rows // BLOCK
    shape = jax.ShapeDtypeStruct((blocks, 1, BLOCK), jnp.float32)
    out = pl.BlockSpec((step // BLOCK, 1, BLOCK), lambda i: (i, 0, 0))
    return pl.pallas_call(
        square_kernel,
        grid=(tok_rows // step,),
        in_specs=[pl.BlockSpec((step, a.shape[1]), lambda i: (i, 0)) for a in (q_raw, key_raw)],
        out_specs=[out, out],
        out_shape=[shape, shape],
        name="row_squares",
    )(q_raw, key_raw)


def from_behind(array, axis, by):
    peers = lax.axis_size(axis)
    pairs = [(i, i + by) for i in range(peers) if 0 <= i + by < peers]
    return lax.ppermute(array, axis, pairs)


def sum_over(array, axis):
    peers = lax.axis_size(axis)
    if peers & (peers - 1):
        return lax.psum(array, axis)
    rounds = peers.bit_length() - 1
    for index in range(rounds):
        moved = lax.ppermute(array, axis, [(i, i ^ (1 << index)) for i in range(peers)])
        array = array + moved
    return array


def whole(query_raw, key_raw, values, output_gradient, query_gain, key_norm_gain, block_docs):
    tok_rows, query_cols = query_raw.shape
    key_cols = key_raw.shape[1]
    kv_heads = key_cols // HEAD_SIZE
    width = query_cols // kv_heads
    tail = tok_rows - WINDOW_REACH
    half = max(1, kv_heads // 2)
    shares = [(0, half)] + ([(half, kv_heads - half)] if kv_heads > half else [])
    halo = from_behind(jnp.concatenate([key_raw[tail:], values[tail:]], axis=1), "ctx", 1)
    q_scale, k_scale = lax.psum(row_squares(query_raw, key_raw), "head")
    halo_scale = from_behind(k_scale[tail // BLOCK :], "ctx", 1)
    q_gain = query_gain.reshape(1, query_cols)
    k_gain = key_norm_gain.reshape(1, key_cols)
    docs = lax.dynamic_slice_in_dim(
        jnp.concatenate([jnp.full((BACK,), -1, jnp.int32), block_docs]),
        lax.axis_index("ctx") * (tok_rows // BLOCK),
        BACK + tok_rows // BLOCK,
        0,
    )

    chunks = tok_rows // WINDOW_REACH
    state = {"rows": [None, None], "gains": None, "dots": None}
    highs, lows, backs, touched = [None] * chunks, [None] * chunks, [], set()

    def run(chunk, share):
        lowest, count = shares[share]
        if chunk == 0:
            lo = (halo, halo_scale, 0, lowest, kv_heads + lowest, halo)
        else:
            lo = (key_raw, k_scale, chunk - 1, lowest, lowest, values)
        passed = state["rows"] + [highs[chunk], state["gains"], state["dots"]]
        if chunk > 0:
            passed.append(lows[chunk])
        result = attention(
            docs, query_raw, q_scale, q_gain, output_gradient,
            lo, (key_raw, k_scale, chunk, lowest, lowest, values),
            k_gain, passed, chunk, (lowest, count), chunk == 0,
            (share in touched, state["dots"] is not None),
        )
        touched.add(share)
        state["rows"] = list(result[:2])
        highs[chunk], state["gains"], state["dots"] = result[2:5]
        if chunk == 0:
            backs.append(from_behind(result[5], "ctx", -1))
        else:
            lows[chunk] = result[5]

    for chunk in range(1, chunks):
        run(chunk, 0)
    for share in range(len(shares)):
        run(0, share)
    for chunk in range(1, chunks):
        for share in range(1, len(shares)):
            run(chunk, share)
    attended, query_scaled = state["rows"]
    dots = add_back_dots(key_raw, k_scale, k_gain, state["dots"], backs)
    dots = lax.psum(dots, "head")
    finished = []
    for share, heads in enumerate(shares):
        finished = list(
            finish(
                query_scaled, query_raw, q_scale, key_raw, k_scale, k_gain,
                dots, highs, lows[1:], backs[share], heads, finished,
            )
        )
    query_grad, key_raw_gradient, value_grad = finished
    gain_grads = sum_over(state["gains"], "ctx").reshape(kv_heads, -1)
    return (
        attended,
        query_grad,
        key_raw_gradient,
        value_grad,
        gain_grads[:, :width].reshape(query_cols),
        gain_grads[:, width:].reshape(key_cols),
    )


def solution(mesh):
    placed = (
        P("ctx", "head"),
        P("ctx", "head"),
        P("ctx", "head"),
        P("ctx", "head"),
        P("head"),
        P("head"),
        P(),
    )
    return jax.shard_map(
        whole,
        mesh=mesh,
        in_specs=placed,
        out_specs=(
            P("ctx", "head"),
            P("ctx", "head"),
            P("ctx", "head"),
            P("ctx", "head"),
            P("head"),
            P("head"),
        ),
        check_vma=False,
    )
```

```python
import functools

import jax
import jax.numpy as jnp
from jax import lax
from jax.experimental import pallas as pl
from jax.experimental.pallas import tpu as pltpu
from jax.sharding import PartitionSpec as P


QUERY_HEADS = 32
KEY_VALUE_HEADS = 8
HEAD_SIZE = 128
WINDOW_REACH = 512
BLOCK = 128

EPS = 1e-06
NEGATIVE = -1e30
LOG2_E = 1.4426950408889634
SOFTMAX_SCALE = HEAD_SIZE ** (-0.5)
VMEM_LIMIT = 16 << 20
SPAN = WINDOW_REACH + BLOCK
BACK = WINDOW_REACH // BLOCK
PAIR = 2 * HEAD_SIZE
PART = BLOCK // 2
PIECES = WINDOW_REACH // PART
REACH = WINDOW_REACH + PART


def on_top(tile, group):
    return jnp.concatenate(
        [tile[:, h * HEAD_SIZE : (h + 1) * HEAD_SIZE] for h in range(group)], axis=0
    )


def as_columns(row):
    return jnp.transpose(jnp.broadcast_to(row, (BLOCK, BLOCK)))


def query_scale(summed):
    return lax.rsqrt(summed * (1.0 / (QUERY_HEADS * HEAD_SIZE)) + EPS)


def key_scale(summed):
    return lax.rsqrt(summed * (1.0 / (KEY_VALUE_HEADS * HEAD_SIZE)) + EPS)


def fold_rows(tile):
    folded = tile[:, :HEAD_SIZE]
    for h in range(1, tile.shape[1] // HEAD_SIZE):
        folded = folded + tile[:, h * HEAD_SIZE : (h + 1) * HEAD_SIZE]
    return jnp.sum(jnp.transpose(folded), axis=0, keepdims=True)


def attention_kernel(group, chunk, chunks, passed, begun, *refs):
    (
        docs_ref,
        q_ref,
        q_scale_ref,
        q_gain_ref,
        grad_ref,
        k_lo_ref,
        k_hi_ref,
        lo_scale_ref,
        hi_scale_ref,
        k_gain_ref,
        v_lo_ref,
        v_hi_ref,
    ) = refs[:12]
    refs = refs[12:]
    prior_gain_ref, prior_dots_ref = None, None
    if begun[0]:
        prior_gain_ref, refs = refs[0], refs[1:]
    if begun[1]:
        prior_dots_ref, refs = refs[0], refs[1:]
    refs = refs[passed:]
    (
        out_ref,
        dq_ref,
        hi_ref,
        gain_grad_ref,
        dots_ref,
        lo_ref,
        k_scr,
        v_scr,
        kt_scr,
        vt_scr,
        unit_scr,
        dk_scr,
        dv_scr,
    ) = refs
    f32, bf16 = jnp.float32, jnp.bfloat16
    q_gain = q_gain_ref[...]
    k_gain = k_gain_ref[...]

    key_total = jnp.zeros((1, HEAD_SIZE), f32)
    key_dots = []

    def prepare(block):
        half, j = divmod(block, BACK)
        raw_ref, scale_ref, val_ref = (
            (k_hi_ref, hi_scale_ref, v_hi_ref) if half else (k_lo_ref, lo_scale_ref, v_lo_ref)
        )
        src = slice(j * BLOCK, (j + 1) * BLOCK)
        dst = slice(block * BLOCK, (block + 1) * BLOCK)
        unit = raw_ref[src, :].astype(f32) * as_columns(key_scale(scale_ref[j]))
        unit_scr[dst, :] = unit
        norm = (unit * k_gain).astype(bf16)
        k_scr[dst, :] = norm
        kt_scr[:, dst] = jnp.transpose(norm)
        vals = val_ref[src, :]
        v_scr[dst, :] = vals
        vt_scr[:, dst] = jnp.transpose(vals)

    def settle(block):
        half, j = divmod(block, BACK)
        ref = hi_ref if half else lo_ref
        dst = slice(j * BLOCK, (j + 1) * BLOCK)
        src = slice(block * BLOCK, (block + 1) * BLOCK)
        dkey = dk_scr[src, :] * SOFTMAX_SCALE
        gained = dkey * unit_scr[src, :]
        key_dots.append(fold_rows(gained * k_gain))
        ref[dst, :HEAD_SIZE] = dkey.astype(ref.dtype)
        ref[dst, HEAD_SIZE:] = dv_scr[src, :].astype(ref.dtype)
        return jnp.sum(gained, axis=0, keepdims=True)

    dk_scr[...] = jnp.zeros_like(dk_scr)
    dv_scr[...] = jnp.zeros_like(dv_scr)

    def mask():
        key_pos = lax.broadcasted_iota(jnp.int32, (PART, lanes), 0)
        query_pos = lax.broadcasted_iota(jnp.int32, (PART, lanes), 1) & (PART - 1)
        return key_pos <= query_pos

    def split_edge(parts):
        causal = mask()
        zero = jnp.zeros_like(parts[0])
        return jnp.concatenate(
            [jnp.where(causal, zero, parts[0])]
            + parts[1:]
            + [jnp.where(causal, parts[0], zero)],
            axis=0,
        ).astype(bf16)

    def pieces(stacked):
        return [stacked[h * PART : (h + 1) * PART] for h in range(group)]

    def unit_of(part):
        step, odd = divmod(part, 2)
        scale = as_columns(query_scale(q_scale_ref[step]))[odd * PART : (odd + 1) * PART]
        raw = q_ref[part * PART : (part + 1) * PART, :].astype(f32)
        return raw * jnp.concatenate([scale] * group, axis=1)

    def in_blocks(part, stacked):
        blank = jnp.zeros((PART, lanes), bf16)
        return jnp.concatenate([blank, stacked] if part % 2 else [stacked, blank], axis=0)

    def forward(part):
        window = slice(part * PART, part * PART + REACH)
        queries = on_top((unit_of(part) * q_gain).astype(bf16), group)
        place = chunk * BACK
        own = docs_ref[place + (part + PIECES) // 2]
        seen = [docs_ref[place + (part + j) // 2] == own for j in range(PIECES)]
        scores = lax.dot_general(
            k_scr[window, :], queries, (((1,), (1,)), ((), ())), preferred_element_type=f32
        )
        piece = [scores[j * PART : (j + 1) * PART] for j in range(PIECES + 1)]
        edge = jnp.where(mask(), piece[PIECES], piece[0] + jnp.where(seen[0], 0.0, NEGATIVE))
        top = jnp.max(edge, axis=0, keepdims=True)
        for j in range(1, PIECES):
            top = jnp.maximum(
                top,
                jnp.max(piece[j], axis=0, keepdims=True) + jnp.where(seen[j], 0.0, NEGATIVE),
            )
        factor = SOFTMAX_SCALE * LOG2_E
        expo = [jnp.exp2((edge - top) * factor)]
        for j in range(1, PIECES):
            lift = top + jnp.where(seen[j], 0.0, -NEGATIVE)
            expo.append(jnp.exp2((piece[j] - lift) * factor))
        total = expo[0]
        for j in range(1, PIECES):
            total = total + expo[j]
        inverse = 1.0 / jnp.sum(total, axis=0, keepdims=True)
        return queries, [e * inverse for e in expo]

    def backward(step, states):
        parts = [2 * step + odd for odd in range(2)]
        windows = [slice(part * PART, part * PART + REACH) for part in parts]
        rows = [slice(part * PART, (part + 1) * PART) for part in parts]
        aligned = slice(step * BLOCK, step * BLOCK + SPAN)
        grads = [on_top(grad_ref[r, :], group) for r in rows]
        grads_t = [jnp.transpose(g) for g in grads]
        weights_low = [split_edge(weights) for _, weights in states]
        both = jnp.concatenate(
            [in_blocks(part, low) for part, low in zip(parts, weights_low)], axis=1
        )
        out_t = jnp.dot(vt_scr[:, aligned], both, preferred_element_type=f32).astype(bf16)
        gains = jnp.zeros((1, group * HEAD_SIZE), f32)
        dlow = []
        for odd in range(2):
            mine = out_t[:, odd * lanes : (odd + 1) * lanes]
            delta = jnp.sum(
                grads_t[odd].astype(f32) * mine.astype(f32), axis=0, keepdims=True
            )
            out_ref[rows[odd], :] = jnp.concatenate(pieces(jnp.transpose(mine)), axis=1)
            dweights = jnp.dot(v_scr[windows[odd], :], grads_t[odd], preferred_element_type=f32)
            dpart = [dweights[j * PART : (j + 1) * PART] for j in range(PIECES + 1)]
            dpart[0] = jnp.where(mask(), dpart[PIECES], dpart[0])
            weights = states[odd][1]
            dlow.append(split_edge([weights[j] * (dpart[j] - delta) for j in range(PIECES)]))
        for odd in range(2):
            dv_scr[windows[odd], :] += jnp.dot(
                weights_low[odd], grads[odd], preferred_element_type=f32
            )
            dk_scr[windows[odd], :] += jnp.dot(
                dlow[odd], states[odd][0], preferred_element_type=f32
            )
        both = jnp.concatenate([in_blocks(part, low) for part, low in zip(parts, dlow)], axis=1)
        dq_t = jnp.dot(kt_scr[:, aligned], both, preferred_element_type=f32)
        for odd in range(2):
            mine = dq_t[:, odd * lanes : (odd + 1) * lanes]
            dquery = jnp.concatenate(pieces(jnp.transpose(mine)), axis=1) * SOFTMAX_SCALE
            unit = unit_of(parts[odd])
            gained = dquery * q_gain
            dq_ref[rows[odd], :] = gained.astype(bf16)
            inner = gained * unit
            folded = inner[:, :HEAD_SIZE]
            for h in range(1, group):
                folded = folded + inner[:, h * HEAD_SIZE : (h + 1) * HEAD_SIZE]
            query_inner.append(folded)
            gains = gains + jnp.sum(dquery * unit, axis=0, keepdims=True)
        return gains

    steps = q_ref.shape[0] // BLOCK
    lanes = group * PART
    query_dots, query_inner = [], []
    total = jnp.zeros((1, group * HEAD_SIZE), f32)
    for block in range(BACK + 1):
        prepare(block)
    states = [forward(0), forward(1)]
    for step in range(steps):
        following = None
        if step + 1 < steps:
            prepare(step + 1 + BACK)
            following = [forward(2 * step + 2), forward(2 * step + 3)]
        total = total + backward(step, states)
        folded = jnp.concatenate(query_inner[-2:], axis=0)
        query_dots.append(jnp.sum(jnp.transpose(folded), axis=0, keepdims=True))
        if step + 1 < steps:
            key_total = key_total + settle(step)
        states = following
    for block in range(steps - 1, 2 * BACK):
        key_total = key_total + settle(block)
    width = group * HEAD_SIZE
    if prior_gain_ref is not None:
        total = total + prior_gain_ref[:, :width]
        key_total = key_total + prior_gain_ref[:, width:]
    gain_grad_ref[:, :width] = total
    gain_grad_ref[:, width:] = key_total

    @pl.when(pl.program_id(0) == 0)
    def _():
        if prior_dots_ref is None:
            dots_ref[...] = jnp.zeros_like(dots_ref)
        else:
            dots_ref[...] = prior_dots_ref[...]

    for step in range(steps):
        dots_ref[chunk * BACK + step] += query_dots[step]
    for j in range(0 if chunk else BACK, 2 * BACK):
        dots_ref[(chunks + chunk - 1) * BACK + j] += key_dots[j]


def attention(
    docs, q_raw, q_scale, q_gain, grad, lo, hi, k_gain, passed, chunk, heads, own_lo, begun
):
    tok_rows, query_cols = q_raw.shape
    key_cols = k_gain.shape[1]
    group = query_cols // key_cols
    width = group * HEAD_SIZE
    lowest, count = heads
    f32, bf16 = jnp.float32, jnp.bfloat16
    rows_spec = pl.BlockSpec((WINDOW_REACH, width), lambda g: (chunk, lowest + g))
    scale_spec = lambda block: pl.BlockSpec((BACK, 1, BLOCK), lambda g: (block, 0, 0))
    key_spec = lambda block, col: pl.BlockSpec((WINDOW_REACH, HEAD_SIZE), lambda g: (block, col + g))
    pair_spec = pl.BlockSpec((WINDOW_REACH, PAIR), lambda g: (0, lowest + g))
    own_pair_spec = pl.BlockSpec((WINDOW_REACH, PAIR), lambda g: (0, g))
    gain_spec = pl.BlockSpec((1, width + HEAD_SIZE), lambda g: (0, lowest + g))
    blocks = tok_rows // BLOCK
    whole_spec = pl.BlockSpec((2 * blocks, 1, BLOCK), lambda g: (0, 0, 0))
    operands = [docs, q_raw, q_scale, q_gain, grad, lo[0], hi[0], lo[1], hi[1], k_gain, lo[5], hi[5]]
    in_specs = [
        pl.BlockSpec(memory_space=pltpu.SMEM),
        rows_spec,
        scale_spec(chunk),
        pl.BlockSpec((1, width), lambda g: (0, lowest + g)),
        rows_spec,
        key_spec(lo[2], lo[3]),
        key_spec(hi[2], hi[3]),
        scale_spec(lo[2]),
        scale_spec(hi[2]),
        pl.BlockSpec((1, HEAD_SIZE), lambda g: (0, lowest + g)),
        key_spec(lo[2] + 1 if own_lo else lo[2], lo[4]),
        key_spec(hi[2], hi[4]),
    ]
    outs = [
        (rows_spec, (tok_rows, query_cols), bf16),
        (rows_spec, (tok_rows, query_cols), bf16),
        (pair_spec, (WINDOW_REACH, 2 * key_cols), bf16),
        (gain_spec, (1, query_cols + key_cols), f32),
        (whole_spec, (2 * blocks, 1, BLOCK), f32),
        (own_pair_spec, (WINDOW_REACH, count * PAIR), bf16)
        if own_lo
        else (pair_spec, (WINDOW_REACH, 2 * key_cols), bf16),
    ]
    aliases, extra = {}, []
    for index, spec in ((3, gain_spec), (4, whole_spec)):
        if begun[index - 3]:
            aliases[len(operands)] = index
            operands.append(passed[index])
            in_specs.append(spec)
    for index, array in enumerate(passed):
        if array is not None and index not in aliases.values():
            aliases[len(operands) + len(extra)] = index
            extra.append(array)
    return pl.pallas_call(
        functools.partial(
            attention_kernel, group, chunk, blocks // BACK, len(extra), begun
        ),
        grid=(count,),
        in_specs=in_specs + [pl.BlockSpec(memory_space=pl.ANY)] * len(extra),
        out_specs=[o[0] for o in outs],
        out_shape=[jax.ShapeDtypeStruct(o[1], o[2]) for o in outs],
        input_output_aliases=aliases,
        scratch_shapes=[
            pltpu.VMEM((2 * WINDOW_REACH, HEAD_SIZE), bf16),
            pltpu.VMEM((2 * WINDOW_REACH, HEAD_SIZE), bf16),
            pltpu.VMEM((HEAD_SIZE, 2 * WINDOW_REACH), bf16),
            pltpu.VMEM((HEAD_SIZE, 2 * WINDOW_REACH), bf16),
            pltpu.VMEM((2 * WINDOW_REACH, HEAD_SIZE), f32),
            pltpu.VMEM((2 * WINDOW_REACH, HEAD_SIZE), f32),
            pltpu.VMEM((2 * WINDOW_REACH, HEAD_SIZE), f32),
        ],
        cost_estimate=pl.CostEstimate(
            flops=12 * WINDOW_REACH * count * width * SPAN,
            bytes_accessed=WINDOW_REACH * count * (8 * width + 16 * HEAD_SIZE),
            transcendentals=WINDOW_REACH * count * group * WINDOW_REACH,
        ),
        name="halo_attention" if own_lo else "attention",
    )(*operands, *extra)


def back_dot_kernel(raw_ref, scale_ref, gain_ref, dots_ref, *refs):
    backs, out_ref = refs[:-1], refs[-1]
    out_ref[...] = dots_ref[...]
    first = dots_ref.shape[0] - BACK
    for j in range(BACK):
        rows = slice(j * BLOCK, (j + 1) * BLOCK)
        index = first + j
        total = jnp.zeros((BLOCK, BLOCK), jnp.float32)
        head = 0
        for back in backs:
            for h in range(back.shape[1] // PAIR):
                cols = slice(head * HEAD_SIZE, (head + 1) * HEAD_SIZE)
                grad = back[rows, h * PAIR : h * PAIR + HEAD_SIZE].astype(jnp.float32)
                total = total + grad * gain_ref[:, cols] * raw_ref[rows, cols].astype(jnp.float32)
                head += 1
        out_ref[index] = dots_ref[index] + fold_rows(total * as_columns(key_scale(scale_ref[j])))


def add_back_dots(key_raw, k_scale, k_gain, dots, backs):
    tok_rows, key_cols = key_raw.shape
    last = tok_rows // WINDOW_REACH - 1
    return pl.pallas_call(
        back_dot_kernel,
        grid=(1,),
        in_specs=[
            pl.BlockSpec((WINDOW_REACH, key_cols), lambda g: (last, 0)),
            pl.BlockSpec((BACK, 1, BLOCK), lambda g: (last, 0, 0)),
            pl.BlockSpec((1, key_cols), lambda g: (0, 0)),
            pl.BlockSpec(dots.shape, lambda g: (0, 0, 0)),
        ]
        + [pl.BlockSpec(back.shape, lambda g: (0, 0)) for back in backs],
        out_specs=pl.BlockSpec(dots.shape, lambda g: (0, 0, 0)),
        out_shape=jax.ShapeDtypeStruct(dots.shape, jnp.float32),
        compiler_params=pltpu.CompilerParams(vmem_limit_bytes=VMEM_LIMIT),
        name="back_dots",
    )(key_raw, k_scale, k_gain, dots, *backs)


def finish_kernel(blocks, chunk, passed, *refs):
    f32 = jnp.float32
    u_ref, q_ref, q_scale_ref, k_ref, k_scale_ref, k_gain_ref, dots_ref, high_ref = refs[:8]
    others, (q_out, k_out, v_out) = refs[8 : len(refs) - 3 - passed], refs[-3:]
    block = chunk * BACK + pl.program_id(0)
    scale = as_columns(query_scale(q_scale_ref[0]))
    dot = as_columns(dots_ref[block] * (1.0 / (QUERY_HEADS * HEAD_SIZE)))
    for h in range(q_ref.shape[1] // HEAD_SIZE):
        cols = slice(h * HEAD_SIZE, (h + 1) * HEAD_SIZE)
        unit = q_ref[:, cols].astype(f32) * scale
        q_out[:, cols] = (scale * (u_ref[:, cols].astype(f32) - unit * dot)).astype(q_out.dtype)
    scale = as_columns(key_scale(k_scale_ref[0]))
    dot = as_columns(dots_ref[blocks + block] * (1.0 / (KEY_VALUE_HEADS * HEAD_SIZE)))
    starts = [(ref, h) for ref in others for h in range(ref.shape[1] // PAIR)]
    for h, (other, place) in enumerate(starts):
        cols = slice(h * HEAD_SIZE, (h + 1) * HEAD_SIZE)
        grad = high_ref[:, h * PAIR : (h + 1) * PAIR].astype(f32)
        grad = grad + other[:, place * PAIR : (place + 1) * PAIR].astype(f32)
        unit = k_ref[:, cols].astype(f32) * scale
        k_out[:, cols] = (
            scale * (grad[:, :HEAD_SIZE] * k_gain_ref[:, cols] - unit * dot)
        ).astype(k_out.dtype)
        v_out[:, cols] = grad[:, HEAD_SIZE:].astype(v_out.dtype)


def finish(scaled, q_raw, q_scale, key_raw, k_scale, k_gain, dots, high, others, chunk, passed):
    tok_rows, query_cols = q_raw.shape
    key_cols = key_raw.shape[1]
    queries = pl.BlockSpec((BLOCK, query_cols), lambda i: (chunk * BACK + i, 0))
    keys = pl.BlockSpec((BLOCK, key_cols), lambda i: (chunk * BACK + i, 0))
    row = pl.BlockSpec((1, 1, BLOCK), lambda i: (chunk * BACK + i, 0, 0))
    pairs = lambda array: pl.BlockSpec((BLOCK, array.shape[1]), lambda i: (i, 0))
    bf16 = jnp.bfloat16
    operands = [scaled, q_raw, q_scale, key_raw, k_scale, k_gain, dots, high, *others]
    return pl.pallas_call(
        functools.partial(finish_kernel, tok_rows // BLOCK, chunk, len(passed)),
        grid=(BACK,),
        in_specs=[
            queries,
            queries,
            row,
            keys,
            row,
            pl.BlockSpec((1, key_cols), lambda i: (0, 0)),
            pl.BlockSpec(dots.shape, lambda i: (0, 0, 0)),
            pairs(high),
        ]
        + [pairs(a) for a in others]
        + [pl.BlockSpec(memory_space=pl.ANY)] * len(passed),
        out_specs=[queries, keys, keys],
        out_shape=[
            jax.ShapeDtypeStruct((tok_rows, query_cols), bf16),
            jax.ShapeDtypeStruct((tok_rows, key_cols), bf16),
            jax.ShapeDtypeStruct((tok_rows, key_cols), bf16),
        ],
        input_output_aliases={len(operands) + i: i for i in range(len(passed))},
        cost_estimate=pl.CostEstimate(
            flops=8 * WINDOW_REACH * query_cols,
            bytes_accessed=WINDOW_REACH * (6 * query_cols + 12 * key_cols),
            transcendentals=0,
        ),
        name="finish",
    )(*operands, *passed)


def from_behind(array, axis, by):
    peers = lax.axis_size(axis)
    pairs = [(i, i + by) for i in range(peers) if 0 <= i + by < peers]
    return lax.ppermute(array, axis, pairs)


def sum_over(array, axis):
    peers = lax.axis_size(axis)
    if peers & (peers - 1):
        return lax.psum(array, axis)
    rounds = peers.bit_length() - 1
    for index in range(rounds):
        moved = lax.ppermute(array, axis, [(i, i ^ (1 << index)) for i in range(peers)])
        array = array + moved
    return array


def whole(query_raw, key_raw, values, output_gradient, query_gain, key_norm_gain, block_docs):
    f32 = jnp.float32
    tok_rows, query_cols = query_raw.shape
    key_cols = key_raw.shape[1]
    kv_heads = key_cols // HEAD_SIZE
    width = query_cols // kv_heads
    tail = tok_rows - WINDOW_REACH
    half = max(1, kv_heads // 2)
    shares = [(0, half)] + ([(half, kv_heads - half)] if kv_heads > half else [])
    halo = from_behind(jnp.concatenate([key_raw[tail:], values[tail:]]), "ctx", 1)
    query_float, key_float = query_raw.astype(f32), key_raw.astype(f32)
    q_scale, k_scale = lax.psum(
        (jnp.sum(query_float * query_float, axis=1), jnp.sum(key_float * key_float, axis=1)),
        "head",
    )
    q_scale = q_scale.reshape(tok_rows // BLOCK, 1, BLOCK)
    k_scale = k_scale.reshape(tok_rows // BLOCK, 1, BLOCK)
    halo_scale = from_behind(k_scale[tail // BLOCK :], "ctx", 1)
    q_gain = query_gain.reshape(1, query_cols)
    k_gain = key_norm_gain.reshape(1, key_cols)
    docs = lax.dynamic_slice_in_dim(
        jnp.concatenate([jnp.full((BACK,), -1, jnp.int32), block_docs]),
        lax.axis_index("ctx") * (tok_rows // BLOCK),
        BACK + tok_rows // BLOCK,
        0,
    )

    chunks = tok_rows // WINDOW_REACH
    state = {"rows": [None, None], "gains": None, "dots": None}
    highs, lows, backs, touched = [None] * chunks, [None] * chunks, [], set()

    def run(chunk, share):
        lowest, count = shares[share]
        if chunk == 0:
            lo = (halo, halo_scale, 0, lowest, lowest, halo)
        else:
            lo = (key_raw, k_scale, chunk - 1, lowest, lowest, values)
        passed = state["rows"] + [highs[chunk], state["gains"], state["dots"]]
        if chunk > 0:
            passed.append(lows[chunk])
        result = attention(
            docs, query_raw, q_scale, q_gain, output_gradient,
            lo, (key_raw, k_scale, chunk, lowest, lowest, values),
            k_gain, passed, chunk, (lowest, count), chunk == 0,
            (share in touched, state["dots"] is not None),
        )
        touched.add(share)
        state["rows"] = list(result[:2])
        highs[chunk], state["gains"], state["dots"] = result[2:5]
        if chunk == 0:
            backs.append(from_behind(result[5], "ctx", -1))
        else:
            lows[chunk] = result[5]

    for chunk in range(1, chunks):
        run(chunk, 0)
    for share in range(len(shares)):
        run(0, share)
    for chunk in range(1, chunks):
        for share in range(1, len(shares)):
            run(chunk, share)
    attended, query_scaled = state["rows"]
    dots = add_back_dots(key_raw, k_scale, k_gain, state["dots"], backs)
    dots = lax.psum(dots, "head")
    finished = []
    for chunk in range(chunks):
        others = [lows[chunk + 1]] if chunk + 1 < chunks else backs
        finished = list(
            finish(
                query_scaled, query_raw, q_scale, key_raw, k_scale, k_gain,
                dots, highs[chunk], others, chunk, finished,
            )
        )
    query_grad, key_raw_gradient, value_grad = finished
    gain_grads = sum_over(state["gains"], "ctx").reshape(kv_heads, -1)
    return (
        attended,
        query_grad,
        key_raw_gradient,
        value_grad,
        gain_grads[:, :width].reshape(query_cols),
        gain_grads[:, width:].reshape(key_cols),
    )


def solution(mesh):
    placed = (
        P("ctx", "head"),
        P("ctx", "head"),
        P("ctx", "head"),
        P("ctx", "head"),
        P("head"),
        P("head"),
        P(),
    )
    return jax.shard_map(
        whole,
        mesh=mesh,
        in_specs=placed,
        out_specs=(
            P("ctx", "head"),
            P("ctx", "head"),
            P("ctx", "head"),
            P("ctx", "head"),
            P("head"),
            P("head"),
        ),
        check_vma=False,
    )
```
